32 devices in a mesh: row: 16 (over z, x, core), feat: 2 (over y).
Axes of the slice: x: 2, y: 2, z: 4, core: 2. Of those that a mesh axis runs over, the one named last changes fastest.
Arguments:
- features: bfloat16 [65536, 8192], P('row', 'feat'), may hold values from -6 to 6
- coef: bfloat16 [8192], P('feat'), may hold values from -0.0625 to 0.0625
- labels: int32 [65536], P('row'), may hold values 0 or 1
- sign_bits: int32 [65536], P('row'), may hold values 0 or 1
- samples: int32 [16, 4096], P('row'), may hold values from 0 to 4095
Outputs:
- gradient: float32 [8192], P('feat')
- sketch: bfloat16 [4096, 8192], P('row', 'feat')
- gram: float32 [4096, 4096], P('row', 'feat')
The draws below stay inside these ranges and needn't reach their ends.
Inputs may be any that keep to these rules, and one draw needn't show every extreme that they name: `samples`: row index inside the block.
All inputs are finite; a program needn't handle non-finite values. No bound on the sum of `labels` or of `sign_bits` on one device may be relied on, other than what follows from the above.
Results may differ from the reference program's by a relative error of at most 0.017.
Values may be sent and summed in bfloat16 or wider, within the bound.
A program may use at most 192 MiB of HBM per device.

```python
import jax
import jax.numpy as jnp
from jax import lax

F = 8192
SKETCH = 4096
ROWS_DEV = 4096
BLOCKS = 16
TOTAL = 65536


def with_ends(values, stream_key, smallest, largest):
    dims = values.shape
    spot = [jax.random.randint(jax.random.fold_in(stream_key, axis), (), 0, dims[axis]) for axis in range(len(dims))]
    values = values.at[tuple(spot)].set(smallest)
    longest = dims.index(max(dims))
    spot[longest] = (spot[longest] + 1) % dims[longest]
    return values.at[tuple(spot)].set(largest)


def block_levels(key, extent, split, low, top_value):
    loudness = 1.0
    for position, shards_of in split:
        heights = jax.random.uniform(jax.random.fold_in(jax.random.fold_in(key, 6), position), (shards_of,), jnp.float32, low / len(split), top_value / len(split))
        loudness = loudness * jnp.repeat(jnp.exp(heights), extent[position] // shards_of).reshape((-1,) + (1,) * (len(extent) - 1 - position))
    return loudness


def gaussian(own_key, extent, spread, bound, shards=(), kind=jnp.bfloat16):
    drawn = jax.random.normal(own_key, extent, jnp.float32) * spread
    if len(shards) > 0:
        drawn = block_levels(own_key, extent, shards, -0.22, 0.18) * drawn
    return jnp.clip(drawn, min=-bound, max=bound).astype(kind)


def setup_inputs(seed: int = 0) -> dict:
    streams_of = jax.random.split(jax.random.key(seed), 6)
    return {
        "features": gaussian(streams_of[0], (TOTAL, F), 1.0, 6.0, ((0, 16), (1, 2))),
        "coef": gaussian(streams_of[1], (F,), F ** -0.5, 0.0625, ((0, 2),)),
        "labels": with_ends((jax.random.randint(streams_of[2], (TOTAL,), 0, 2) < 1).astype(jnp.int32), jax.random.fold_in(streams_of[2], 1), 0, 1),
        "sign_bits": with_ends((jax.random.randint(streams_of[3], (TOTAL,), 0, 2) < 1).astype(jnp.int32), jax.random.fold_in(streams_of[3], 1), 0, 1),
        "samples": with_ends(jax.random.randint(streams_of[4], (BLOCKS, SKETCH), 0, ROWS_DEV), jax.random.fold_in(streams_of[4], 1), 0, ROWS_DEV - 1).astype(jnp.int32),
    }


def sylvester(hadamard_order):
    positions = jnp.arange(hadamard_order, dtype=jnp.int32)
    bit_correlation = positions[:, None] & positions[None, :]
    parity_count = jnp.zeros_like(bit_correlation)
    for bit_pos in range(max(hadamard_order.bit_length() - 1, 0)):
        parity_count = parity_count + (bit_correlation >> bit_pos & 1)
    return (1 - 2 * (parity_count % 2)).astype(jnp.float32)

def transform_block(block_rows):
    big_order = 32
    small_order = block_rows.shape[0] // big_order
    high_table = sylvester(big_order)
    low_table = sylvester(small_order)
    shaped = block_rows.reshape(big_order, small_order, block_rows.shape[1])
    first_pass = jnp.einsum('ij,jkf->ikf', high_table, shaped, precision=lax.Precision.HIGHEST)
    second_pass = jnp.einsum('kl,ilf->ikf', low_table, first_pass, precision=lax.Precision.HIGHEST)
    return second_pass.reshape(block_rows.shape[0], block_rows.shape[1])

def reference(features, coef, labels, sign_bits, samples):
    margins = jnp.dot(features, coef, preferred_element_type=jnp.float32)
    probability = jax.nn.sigmoid(margins)
    row_scale = jnp.sqrt(probability * (1.0 - probability))
    residual = (probability - labels.astype(jnp.float32)).astype(jnp.bfloat16)
    root_total = jnp.sqrt(jnp.float32(TOTAL))
    gradient = jnp.dot(residual, features, preferred_element_type=jnp.float32) / root_total
    factors = (2.0 * sign_bits.astype(jnp.float32) - 1.0) * row_scale
    blocks = features.reshape(BLOCKS, ROWS_DEV, F)
    factor_blocks = factors.reshape(BLOCKS, ROWS_DEV)

    def add_block(carry, inputs):
        block_rows, block_factor, block_samples = inputs
        weighted = (block_factor[:, None] * block_rows.astype(jnp.float32)).astype(jnp.bfloat16)
        transformed = transform_block(weighted.astype(jnp.float32))
        picked = lax.optimization_barrier(jnp.take(transformed, block_samples, axis=0).astype(jnp.bfloat16))
        return (carry + picked.astype(jnp.float32), None)
    total_sum, unused = lax.scan(add_block, jnp.zeros((SKETCH, F), jnp.float32), (blocks, factor_blocks, samples))
    sketch = (total_sum / root_total).astype(jnp.bfloat16)
    gram = jnp.dot(sketch, sketch.T, preferred_element_type=jnp.float32) / F
    return (gradient, sketch, gram)
```

```python
import functools

import jax
import jax.numpy as jnp
from jax import lax
from jax.experimental import pallas as pl
from jax.experimental.pallas import tpu as pltpu
from jax.sharding import PartitionSpec as P

VMEM_BYTES = 48 << 20


def hadamard(n):
    a = lax.broadcasted_iota(jnp.int32, (n, n), 0)
    b = lax.broadcasted_iota(jnp.int32, (n, n), 1)
    return (1 - 2 * (lax.population_count(a & b) & 1)).astype(jnp.bfloat16)


def transform_kernel(low, slab, table_ref, factor_ref, x_ref, out_ref, wide, mid):
    rows, width = x_ref.shape
    high = rows // low
    lanes = wide.shape[1]

    @pl.when(pl.program_id(0) == 0)
    def _():
        wide[...] = jnp.broadcast_to(factor_ref[...], wide.shape)

    table = table_ref[...]
    for k in range(high):
        span = pl.ds(k * low, low)
        scale = wide[span, :]
        parts = [
            (scale * x_ref[span, pl.ds(c, lanes)].astype(jnp.float32)).astype(
                jnp.bfloat16
            )
            for c in range(0, width, lanes)
        ]
        weighted = jnp.concatenate(parts, axis=1)
        mid[k] = jnp.dot(table, weighted, preferred_element_type=jnp.float32)

    @pl.loop(0, low // slab)
    def _(i):
        at = pl.multiple_of(i * slab, slab)
        vals = [mid[k, pl.ds(at, slab), :] for k in range(high)]
        step = 1
        while step < high:
            vals = [
                vals[k ^ step] - vals[k] if k & step else vals[k] + vals[k ^ step]
                for k in range(high)
            ]
            step *= 2
        for k in range(high):
            out_ref[pl.ds(k * low + at, slab), :] = vals[k]


def transform(features, factor, first, count):
    rows = features.shape[0]
    low, width = min(256, rows), min(256, count)
    return pl.pallas_call(
        functools.partial(transform_kernel, low, 8),
        out_shape=jax.ShapeDtypeStruct((rows, count), jnp.float32),
        grid=(count // width,),
        in_specs=[
            pl.BlockSpec((low, low), lambda i: (0, 0)),
            pl.BlockSpec((rows, 1), lambda i: (0, 0)),
            pl.BlockSpec((rows, width), lambda i: (0, i + first // width)),
        ],
        out_specs=pl.BlockSpec((rows, width), lambda i: (0, i)),
        scratch_shapes=[
            pltpu.VMEM((rows, 128), jnp.float32),
            pltpu.VMEM((rows // low, low, width), jnp.float32),
        ],
        compiler_params=pltpu.CompilerParams(vmem_limit_bytes=VMEM_BYTES),
        cost_estimate=pl.CostEstimate(
            flops=2 * rows * count * low,
            bytes_accessed=rows * count * 8,
            transcendentals=0,
        ),
        name="transform",
    )(hadamard(low), factor, features)


def gather_kernel(tile, index_ref, table_ref, out_ref, held, sem):
    i = pl.program_id(0)
    steps = pl.num_programs(0)

    def fetch(step, slot):
        for r in range(tile):
            pltpu.make_async_copy(
                table_ref.at[pl.ds(index_ref[step * tile + r], 1), :],
                held.at[slot, pl.ds(r, 1), :],
                sem.at[slot],
            ).start()

    @pl.when(i == 0)
    def _():
        fetch(0, 0)

    @pl.when(i + 1 < steps)
    def _():
        fetch(i + 1, lax.rem(i + 1, 2))

    slot = lax.rem(i, 2)
    pltpu.make_async_copy(
        table_ref.at[pl.ds(0, tile), :], held.at[slot], sem.at[slot]
    ).wait()
    out_ref[...] = held[slot].astype(jnp.bfloat16)


def gather(table, index):
    rows, width = index.shape[0], table.shape[1]
    tile = min(128, rows)
    return pl.pallas_call(
        functools.partial(gather_kernel, tile),
        out_shape=jax.ShapeDtypeStruct((rows, width), jnp.bfloat16),
        grid_spec=pltpu.PrefetchScalarGridSpec(
            num_scalar_prefetch=1,
            grid=(rows // tile,),
            in_specs=[pl.BlockSpec(memory_space=pl.ANY)],
            out_specs=pl.BlockSpec((tile, width), lambda i, index: (i, 0)),
            scratch_shapes=[
                pltpu.VMEM((2, tile, width), jnp.float32),
                pltpu.SemaphoreType.DMA((2,)),
            ],
        ),
        compiler_params=pltpu.CompilerParams(vmem_limit_bytes=VMEM_BYTES),
        cost_estimate=pl.CostEstimate(
            flops=0, bytes_accessed=rows * width * 8, transcendentals=0
        ),
        name="gather",
    )(index, table)


def ring_order(n):
    if n % 4:
        return list(range(n))
    out = [4 * z + c for z in range(n // 4) for c in (0, 1)]
    back = [4 * z + c for z in reversed(range(n // 4)) for c in (2, 3)]
    return out + back


def sum_over(value, axis):
    n = lax.axis_size(axis)
    if n & (n - 1):
        return lax.psum(value, axis)
    step = 1
    while step < n:
        value = value + lax.ppermute(value, axis, [(i, i ^ step) for i in range(n)])
        step *= 2
    return value


def per_device(features, coef, labels, sign_bits, samples):
    n = lax.axis_size("row")
    groups = lax.axis_size("feat")
    rows_here, feat_here = features.shape
    all_features = feat_here * groups
    root_total = jnp.sqrt(jnp.float32(rows_here * n))
    order = ring_order(n)
    cw = [(order[i], order[(i + 1) % n]) for i in range(n)]
    ccw = [(order[(i + 1) % n], order[i]) for i in range(n)]
    place = [0] * n
    for i, device in enumerate(order):
        place[device] = i
    me = lax.axis_index("row")
    pos = jnp.asarray(place, jnp.int32)[me]
    order_table = jnp.asarray(order, jnp.int32)

    margins = sum_over(
        jnp.dot(features, coef, preferred_element_type=jnp.float32), "feat"
    )
    probability = jax.nn.sigmoid(margins)
    row_scale = jnp.sqrt(probability * (1.0 - probability))
    residual = (probability - labels.astype(jnp.float32)).astype(jnp.bfloat16)
    signs = 2.0 * sign_bits.astype(jnp.float32) - 1.0
    factor = (signs * row_scale)[:, None]
    half = feat_here // 2

    depth = samples.shape[1] // n
    owners = order_table[(pos + jnp.arange(n, dtype=jnp.int32)) % n]
    near = jnp.take(samples[0].reshape(n, depth), owners, axis=0)

    def add(*terms):
        total = terms[0].astype(jnp.float32)
        for term in terms[1:]:
            total = total + term.astype(jnp.float32)
        return total

    h = n // 2
    pairs = [jnp.concatenate([near[h - s], near[(s - h + 1) % n]]) for s in range(h)]
    sides = (0, 1)
    tables, rows = [], [pairs[0]] * 2
    for side in sides:
        tables.append(transform(features, factor, side * half, half))
        if not side:
            tables[0], factor = lax.optimization_barrier((tables[0], factor))
    ahead_in, behind_in, own = [None] * 2, [None] * 2, [None] * 2
    for s in range(h):
        for side in sides:
            both = gather(tables[side], rows[side])
            ahead, behind = both[:depth], both[depth:]
            if s:
                ahead = add(ahead, ahead_in[side]).astype(jnp.bfloat16)
            if s < h - 1:
                if s:
                    behind = add(behind, behind_in[side]).astype(jnp.bfloat16)
                ahead, behind, rows[side] = lax.optimization_barrier(
                    (ahead, behind, pairs[s + 1])
                )
                behind_in[side] = lax.ppermute(behind, "row", ccw)
            else:
                own[side] = behind
            if s == 2 and side:
                ahead, residual = lax.optimization_barrier((ahead, residual))
            ahead_in[side] = lax.ppermute(ahead, "row", cw)
    parts = []
    for side in sides:
        total = add(own[side], ahead_in[side], behind_in[side])
        parts.append((total / root_total).astype(jnp.bfloat16))
    sketch = jnp.concatenate(parts, axis=1)
    long_perm, short_perm = (cw, ccw), (ccw, cw)
    sign = (1, -1)

    grad_total = jnp.dot(residual, features, preferred_element_type=jnp.float32)
    gradient = sum_over(grad_total, "row") / root_total

    blocks = [{0: parts[0]}, {0: parts[1]}]
    grams, others = {}, {}
    swap = [(0, 1), (1, 0)]

    def gram_of(distance):
        a, b = blocks[0][distance], blocks[1][distance]
        dims = (((1,), (1,)), ((), ()))
        return lax.dot_general(
            parts[0], a, dims, preferred_element_type=jnp.float32
        ) + lax.dot_general(parts[1], b, dims, preferred_element_type=jnp.float32)

    def finish(distances):
        for d in distances:
            grams[d] = gram_of(d)
        if groups == 2:
            sent = jnp.concatenate(
                [grams[d].astype(jnp.bfloat16) for d in distances], axis=0
            )
            got = lax.ppermute(sent, "feat", swap)
            for i, d in enumerate(distances):
                others[d] = got[i * depth : (i + 1) * depth]

    for s in range(h):
        for side in (0, 1):
            prev, here = (-sign[side] * s) % n, (-sign[side] * (s + 1)) % n
            blocks[side][here] = lax.ppermute(
                blocks[side][prev], "row", long_perm[side]
            )
            if s < h - 1:
                prev, here = (sign[side] * s) % n, (sign[side] * (s + 1)) % n
                blocks[side][here] = lax.ppermute(
                    blocks[side][prev], "row", short_perm[side]
                )
        if s == 0:
            finish([0])
        if s < h - 1:
            finish([(s + 1) % n, (-s - 1) % n])
        else:
            finish([h])

    where = (jnp.asarray(place, jnp.int32) - pos) % n
    if groups == 2:
        stacked = jnp.stack([add(grams[d], others[d]) for d in range(n)])
        wanted = n // groups
        feat = lax.axis_index("feat")
        mine = lax.dynamic_slice_in_dim(where, feat * wanted, wanted)
        block = jnp.take(stacked, mine, axis=0) / all_features
        gram_block = block.transpose(1, 0, 2).reshape(depth, wanted * depth)
    else:
        stacked = jnp.stack([grams[d].astype(jnp.bfloat16) for d in range(n)])
        part = jnp.take(stacked, where, axis=0)
        part = part.transpose(1, 0, 2).reshape(depth, n * depth)
        gram_block = (
            lax.psum_scatter(part, "feat", scatter_dimension=1, tiled=True).astype(
                jnp.float32
            )
            / all_features
        )
    return (gradient, sketch, gram_block)


def solution(mesh):
    in_specs = (P("row", "feat"), P("feat"), P("row"), P("row"), P("row", None))
    out_specs = (P("feat"), P("row", "feat"), P("row", "feat"))
    return jax.shard_map(
        per_device, mesh=mesh, in_specs=in_specs, out_specs=out_specs, check_vma=False
    )
```

```python
import functools

import jax
import jax.numpy as jnp
from jax import lax
from jax.experimental import pallas as pl
from jax.experimental.pallas import tpu as pltpu
from jax.sharding import PartitionSpec as P

VMEM_BYTES = 48 << 20


def hadamard(n):
    a = lax.broadcasted_iota(jnp.int32, (n, n), 0)
    b = lax.broadcasted_iota(jnp.int32, (n, n), 1)
    return (1 - 2 * (lax.population_count(a & b) & 1)).astype(jnp.bfloat16)


def transform_kernel(low, slab, table_ref, factor_ref, x_ref, out_ref, wide, mid):
    rows, width = x_ref.shape
    high = rows // low
    lanes = wide.shape[1]

    @pl.when(pl.program_id(0) == 0)
    def _():
        wide[...] = jnp.broadcast_to(factor_ref[...], wide.shape)

    table = table_ref[...]
    for k in range(high):
        span = pl.ds(k * low, low)
        scale = wide[span, :]
        parts = [
            (scale * x_ref[span, pl.ds(c, lanes)].astype(jnp.float32)).astype(
                jnp.bfloat16
            )
            for c in range(0, width, lanes)
        ]
        weighted = jnp.concatenate(parts, axis=1)
        mid[k] = jnp.dot(table, weighted, preferred_element_type=jnp.float32)

    @pl.loop(0, low // slab)
    def _(i):
        at = pl.multiple_of(i * slab, slab)
        vals = [mid[k, pl.ds(at, slab), :] for k in range(high)]
        step = 1
        while step < high:
            vals = [
                vals[k ^ step] - vals[k] if k & step else vals[k] + vals[k ^ step]
                for k in range(high)
            ]
            step *= 2
        for k in range(high):
            out_ref[pl.ds(k * low + at, slab), :] = vals[k]


def transform(features, factor, first, count):
    rows = features.shape[0]
    low, width = min(256, rows), min(256, count)
    return pl.pallas_call(
        functools.partial(transform_kernel, low, 8),
        out_shape=jax.ShapeDtypeStruct((rows, count), jnp.float32),
        grid=(count // width,),
        in_specs=[
            pl.BlockSpec((low, low), lambda i: (0, 0)),
            pl.BlockSpec((rows, 1), lambda i: (0, 0)),
            pl.BlockSpec((rows, width), lambda i: (0, i + first // width)),
        ],
        out_specs=pl.BlockSpec((rows, width), lambda i: (0, i)),
        scratch_shapes=[
            pltpu.VMEM((rows, 128), jnp.float32),
            pltpu.VMEM((rows // low, low, width), jnp.float32),
        ],
        compiler_params=pltpu.CompilerParams(vmem_limit_bytes=VMEM_BYTES),
        cost_estimate=pl.CostEstimate(
            flops=2 * rows * count * low,
            bytes_accessed=rows * count * 8,
            transcendentals=0,
        ),
        name="transform",
    )(hadamard(low), factor, features)


def gather_kernel(tile, index_ref, table_ref, out_ref, held, sem):
    i = pl.program_id(0)
    steps = pl.num_programs(0)

    def fetch(step, slot):
        for r in range(tile):
            pltpu.make_async_copy(
                table_ref.at[pl.ds(index_ref[step * tile + r], 1), :],
                held.at[slot, pl.ds(r, 1), :],
                sem.at[slot],
            ).start()

    @pl.when(i == 0)
    def _():
        fetch(0, 0)

    @pl.when(i + 1 < steps)
    def _():
        fetch(i + 1, lax.rem(i + 1, 2))

    slot = lax.rem(i, 2)
    pltpu.make_async_copy(
        table_ref.at[pl.ds(0, tile), :], held.at[slot], sem.at[slot]
    ).wait()
    out_ref[...] = held[slot].astype(jnp.bfloat16)


def gather(table, index):
    rows, width = index.shape[0], table.shape[1]
    tile = min(128, rows)
    return pl.pallas_call(
        functools.partial(gather_kernel, tile),
        out_shape=jax.ShapeDtypeStruct((rows, width), jnp.bfloat16),
        grid_spec=pltpu.PrefetchScalarGridSpec(
            num_scalar_prefetch=1,
            grid=(rows // tile,),
            in_specs=[pl.BlockSpec(memory_space=pl.ANY)],
            out_specs=pl.BlockSpec((tile, width), lambda i, index: (i, 0)),
            scratch_shapes=[
                pltpu.VMEM((2, tile, width), jnp.float32),
                pltpu.SemaphoreType.DMA((2,)),
            ],
        ),
        compiler_params=pltpu.CompilerParams(vmem_limit_bytes=VMEM_BYTES),
        cost_estimate=pl.CostEstimate(
            flops=0, bytes_accessed=rows * width * 8, transcendentals=0
        ),
        name="gather",
    )(index, table)


MESH = pl.DeviceIdType.MESH


def device_at(place, n):
    place = lax.rem(place + n, n)
    back = place - n // 2
    ahead = 4 * lax.div(place, 2) + lax.rem(place, 2)
    behind = 4 * (n // 4 - 1 - lax.div(back, 2)) + 2 + lax.rem(back, 2)
    return jnp.where(back < 0, ahead, behind)


def place_of(device, n):
    z, c = lax.div(device, 4), lax.rem(device, 4)
    return jnp.where(c < 2, 2 * z + c, n // 2 + 2 * (n // 4 - 1 - z) + c - 2)


def gram_kernel(
    n,
    cut,
    a_ref,
    b_ref,
    out_ref,
    held,
    total,
    turned,
    turned_in,
    half,
    half_in,
    hop_send,
    hop_recv,
    turn_send,
    turn_recv,
    half_send,
    half_recv,
):
    h = n // 2
    depth = a_ref.shape[0]
    piece = depth // cut
    row, feat = lax.axis_index("row"), lax.axis_index("feat")
    place = place_of(row, n)
    own = (a_ref, b_ref)
    onward = (device_at(place + 1, n), device_at(place - 1, n))
    dims = (((1,), (1,)), ((), ()))

    barrier = pltpu.get_barrier_semaphore()

    @pl.loop(1, h)
    def _(s):
        for other in (device_at(place + s, n), device_at(place - s, n)):
            pl.semaphore_signal(
                barrier, inc=1, device_id=(other, feat), device_id_type=MESH
            )

    pl.semaphore_signal(barrier, inc=1, device_id=(row, 1 - feat), device_id_type=MESH)
    pl.semaphore_wait(barrier, 2 * (h - 1) + 1)

    def hop(side, slot, i, source):
        span = pl.ds(i * piece, piece)
        return pltpu.make_async_remote_copy(
            src_ref=source.at[span, :],
            dst_ref=held.at[side, slot, span, :],
            send_sem=hop_send.at[side, slot, i],
            recv_sem=hop_recv.at[side, slot, i],
            device_id=(onward[side], feat),
            device_id_type=MESH,
        )

    def turn(side, s):
        target = device_at(place + (s if side else -s), n)
        return pltpu.make_async_remote_copy(
            src_ref=turned.at[side, s],
            dst_ref=turned_in.at[side, s],
            send_sem=turn_send.at[side, s],
            recv_sem=turn_recv.at[side, s],
            device_id=(target, feat),
            device_id_type=MESH,
        )

    def across(d):
        return pltpu.make_async_remote_copy(
            src_ref=half.at[d],
            dst_ref=half_in.at[d],
            send_sem=half_send.at[d],
            recv_sem=half_recv.at[d],
            device_id=(row, 1 - feat),
            device_id_type=MESH,
        )

    def column(d):
        return device_at(place + d, n)

    def mine(d):
        return lax.div(column(d), h) == feat

    def product(left, right):
        return lax.dot_general(left, right, dims, preferred_element_type=jnp.float32)

    def settle(d, value):
        keep = mine(d)

        @pl.when(keep)
        def _():
            total[d] = value

        @pl.when(jnp.logical_not(keep))
        def _():
            half[d] = value.astype(jnp.bfloat16)
            across(d).start()

    def join(s):
        turn(0, s).wait_recv()
        settle(s, total[s] + turned_in[0, s].astype(jnp.float32))
        turn(1, s).wait_recv()
        settle(n - s, total[n - s] + turned_in[1, s].astype(jnp.float32))

    for i in range(cut):
        for side in (0, 1):
            hop(side, 0, i, own[side]).start()
    settle(0, product(a_ref[...], a_ref[...]) + product(b_ref[...], b_ref[...]))

    @pl.loop(1, h)
    def _(s):
        slot = s - 1
        for i in range(cut):
            for side in (0, 1):
                hop(side, slot, i, own[side]).wait_recv()
                hop(side, s, i, held.at[side, slot]).start()
        for side in (0, 1):
            block = held[side, slot]
            turned[side, s] = product(block, own[side][...]).astype(jnp.bfloat16)
            turn(side, s).start()
        total[n - s] = product(a_ref[...], held[0, slot])
        total[s] = product(b_ref[...], held[1, slot])

        @pl.when(s > 2)
        def _():
            join(s - 2)

    for i in range(cut):
        for side in (0, 1):
            hop(side, h - 1, i, own[side]).wait_recv()
    settle(h, product(a_ref[...], held[0, h - 1]) + product(b_ref[...], held[1, h - 1]))
    for s in range(max(h - 2, 1), h):
        join(s)

    @pl.loop(0, n)
    def _(d):
        keep = mine(d)

        @pl.when(keep)
        def _():
            across(d).wait_recv()
            at = pl.multiple_of((column(d) - feat * h) * depth, depth)
            out_ref[:, pl.ds(at, depth)] = total[d] + half_in[d].astype(jnp.float32)

        @pl.when(jnp.logical_not(keep))
        def _():
            across(d).wait_send()

    @pl.loop(0, h)
    def _(s):
        for side in (0, 1):
            for i in range(cut):
                hop(side, s, i, own[side]).wait_send()

            @pl.when(s > 0)
            def _():
                turn(side, s).wait_send()


def paired_gram(a, b, n):
    depth, width = a.shape
    h, cut = n // 2, 2
    return pl.pallas_call(
        functools.partial(gram_kernel, n, cut),
        out_shape=jax.ShapeDtypeStruct((depth, h * depth), jnp.float32),
        in_specs=[pl.BlockSpec(memory_space=pltpu.VMEM)] * 2,
        out_specs=pl.BlockSpec(memory_space=pltpu.VMEM),
        scratch_shapes=[
            pltpu.VMEM((2, h, depth, width), jnp.bfloat16),
            pltpu.VMEM((n, depth, depth), jnp.float32),
            pltpu.VMEM((2, h, depth, depth), jnp.bfloat16),
            pltpu.VMEM((2, h, depth, depth), jnp.bfloat16),
            pltpu.VMEM((n, depth, depth), jnp.bfloat16),
            pltpu.VMEM((n, depth, depth), jnp.bfloat16),
            pltpu.SemaphoreType.DMA((2, h, cut)),
            pltpu.SemaphoreType.DMA((2, h, cut)),
            pltpu.SemaphoreType.DMA((2, h)),
            pltpu.SemaphoreType.DMA((2, h)),
            pltpu.SemaphoreType.DMA((n,)),
            pltpu.SemaphoreType.DMA((n,)),
        ],
        compiler_params=pltpu.CompilerParams(
            collective_id=0, has_side_effects=True, vmem_limit_bytes=VMEM_BYTES
        ),
        name="paired_gram",
    )(a, b)


def ring_order(n):
    if n % 4:
        return list(range(n))
    out = [4 * z + c for z in range(n // 4) for c in (0, 1)]
    back = [4 * z + c for z in reversed(range(n // 4)) for c in (2, 3)]
    return out + back


def sum_over(value, axis):
    n = lax.axis_size(axis)
    if n & (n - 1):
        return lax.psum(value, axis)
    step = 1
    while step < n:
        value = value + lax.ppermute(value, axis, [(i, i ^ step) for i in range(n)])
        step *= 2
    return value


def per_device(features, coef, labels, sign_bits, samples):
    n = lax.axis_size("row")
    groups = lax.axis_size("feat")
    rows_here, feat_here = features.shape
    all_features = feat_here * groups
    root_total = jnp.sqrt(jnp.float32(rows_here * n))
    order = ring_order(n)
    cw = [(order[i], order[(i + 1) % n]) for i in range(n)]
    ccw = [(order[(i + 1) % n], order[i]) for i in range(n)]
    place = [0] * n
    for i, device in enumerate(order):
        place[device] = i
    me = lax.axis_index("row")
    pos = jnp.asarray(place, jnp.int32)[me]
    order_table = jnp.asarray(order, jnp.int32)

    margins = sum_over(
        jnp.dot(features, coef, preferred_element_type=jnp.float32), "feat"
    )
    probability = jax.nn.sigmoid(margins)
    row_scale = jnp.sqrt(probability * (1.0 - probability))
    residual = (probability - labels.astype(jnp.float32)).astype(jnp.bfloat16)
    signs = 2.0 * sign_bits.astype(jnp.float32) - 1.0
    factor = (signs * row_scale)[:, None]
    half = feat_here // 2

    depth = samples.shape[1] // n
    owners = order_table[(pos + jnp.arange(n, dtype=jnp.int32)) % n]
    near = jnp.take(samples[0].reshape(n, depth), owners, axis=0)

    def add(*terms):
        total = terms[0].astype(jnp.float32)
        for term in terms[1:]:
            total = total + term.astype(jnp.float32)
        return total

    h = n // 2
    sides = (0, 1)
    pairs = [
        [jnp.concatenate([near[h - s], near[(s - h + 1) % n]]) for s in range(h)],
        [jnp.concatenate([near[(s - h) % n], near[h - s - 1]]) for s in range(h)],
    ]
    long_perm, short_perm = (cw, ccw), (ccw, cw)
    streams = ((0, half // 2, 0), (half // 2, half // 2, 0), (half, half, 1))
    count = len(streams)
    grad, grad_in, shift = None, None, 1

    def turn(value, shift):
        return lax.ppermute(value, "row", [(i, i ^ shift) for i in range(n)])

    tables, rows = [], []
    for first, width, side in streams:
        tables.append(transform(features, factor, first, width))
        rows.append(pairs[side][0])
        tables[-1], factor = lax.optimization_barrier((tables[-1], factor))
    ahead_in, behind_in, own = [None] * count, [None] * count, [None] * count
    for s in range(h):
        for k, (_, _, side) in enumerate(streams):
            both = gather(tables[k], rows[k])
            ahead, behind = both[:depth], both[depth:]
            if s:
                ahead = add(ahead, ahead_in[k]).astype(jnp.bfloat16)
            if s < h - 1:
                if s:
                    behind = add(behind, behind_in[k]).astype(jnp.bfloat16)
                ahead, behind, rows[k] = lax.optimization_barrier(
                    (ahead, behind, pairs[side][s + 1])
                )
                behind_in[k] = lax.ppermute(behind, "row", short_perm[side])
            else:
                own[k] = behind
            ahead_in[k] = lax.ppermute(ahead, "row", long_perm[side])
        if s == 1:
            residual, rows[0] = lax.optimization_barrier((residual, rows[0]))
            grad = jnp.dot(residual, features, preferred_element_type=jnp.float32)
            grad, rows[-1] = lax.optimization_barrier((grad, rows[-1]))
            grad_in = turn(grad, shift)
        elif s > 1 and s < h - 1 and shift < n:
            grad = grad + grad_in
            shift *= 2
            grad, rows[-1] = lax.optimization_barrier((grad, rows[-1]))
            if shift < n:
                grad_in = turn(grad, shift)
    while shift < n:
        grad = grad + grad_in
        shift *= 2
        if shift < n:
            grad_in = turn(grad, shift)
    gradient = grad / root_total
    parts = [[], []]
    for k, (_, _, side) in enumerate(streams):
        total = add(own[k], ahead_in[k], behind_in[k])
        parts[side].append((total / root_total).astype(jnp.bfloat16))
    parts = [jnp.concatenate(part, axis=1) for part in parts]
    sketch = jnp.concatenate(parts, axis=1)
    sign = (1, -1)

    if groups == 2 and n % 4 == 0 and n >= 8:
        gram_block = paired_gram(parts[0], parts[1], n) / all_features
        return (gradient, sketch, gram_block)

    blocks = [{0: parts[0]}, {0: parts[1]}]
    grams, others = {}, {}
    swap = [(0, 1), (1, 0)]

    def gram_of(distance):
        a, b = blocks[0][distance], blocks[1][distance]
        dims = (((1,), (1,)), ((), ()))
        return lax.dot_general(
            parts[0], a, dims, preferred_element_type=jnp.float32
        ) + lax.dot_general(parts[1], b, dims, preferred_element_type=jnp.float32)

    def finish(distances):
        for d in distances:
            grams[d] = gram_of(d)
        if groups == 2:
            sent = jnp.concatenate(
                [grams[d].astype(jnp.bfloat16) for d in distances], axis=0
            )
            got = lax.ppermute(sent, "feat", swap)
            for i, d in enumerate(distances):
                others[d] = got[i * depth : (i + 1) * depth]

    for s in range(h):
        for side in (0, 1):
            prev, here = (-sign[side] * s) % n, (-sign[side] * (s + 1)) % n
            blocks[side][here] = lax.ppermute(
                blocks[side][prev], "row", long_perm[side]
            )
            if s < h - 1:
                prev, here = (sign[side] * s) % n, (sign[side] * (s + 1)) % n
                blocks[side][here] = lax.ppermute(
                    blocks[side][prev], "row", short_perm[side]
                )
        if s == 0:
            finish([0])
        if s < h - 1:
            finish([(s + 1) % n, (-s - 1) % n])
        else:
            finish([h])

    where = (jnp.asarray(place, jnp.int32) - pos) % n
    if groups == 2:
        stacked = jnp.stack([add(grams[d], others[d]) for d in range(n)])
        wanted = n // groups
        feat = lax.axis_index("feat")
        mine = lax.dynamic_slice_in_dim(where, feat * wanted, wanted)
        block = jnp.take(stacked, mine, axis=0) / all_features
        gram_block = block.transpose(1, 0, 2).reshape(depth, wanted * depth)
    else:
        stacked = jnp.stack([grams[d].astype(jnp.bfloat16) for d in range(n)])
        part = jnp.take(stacked, where, axis=0)
        part = part.transpose(1, 0, 2).reshape(depth, n * depth)
        gram_block = (
            lax.psum_scatter(part, "feat", scatter_dimension=1, tiled=True).astype(
                jnp.float32
            )
            / all_features
        )
    return (gradient, sketch, gram_block)


def solution(mesh):
    in_specs = (P("row", "feat"), P("feat"), P("row"), P("row"), P("row", None))
    out_specs = (P("feat"), P("row", "feat"), P("row", "feat"))
    return jax.shard_map(
        per_device, mesh=mesh, in_specs=in_specs, out_specs=out_specs, check_vma=False
    )
```
